32 devices in a mesh: expert: 16 (over z, y, x), mp: 2 (over core).
Axes of the slice: x: 2, y: 2, z: 4, core: 2. Of those that a mesh axis runs over, the one named last changes fastest.
Arguments:
- tokens: bfloat16 [256, 4096], P('expert'), may hold values from -8 to 8
- norm_gain: bfloat16 [4096], replicated, may hold values from 0.25 to 1.75
- expert_ids: int32 [256, 1], P('expert'), may hold values from 0 to 15; in each aligned block of 16 rows (0 to 15, 16 to 31, ...) at most 2 rows name the same one
- w_in: bfloat16 [16, 4096, 2048], P('expert', None, 'mp'), may hold values from -0.09375 to 0.09375
- w_out: bfloat16 [16, 2048, 4096], P('expert', 'mp'), may hold values from -0.125 to 0.125
- queries: bfloat16 [256, 2048], P('expert', 'mp'), may hold values from -4.5 to 4.5
- keys: bfloat16 [256, 128, 512], P('expert', None, 'mp'), may hold values from -4.5 to 4.5
- values: bfloat16 [256, 128, 512], P('expert', None, 'mp'), may hold values from -6 to 6
- new_keys: bfloat16 [256, 512], P('expert', 'mp'), may hold values from -9 to 9
- new_values: bfloat16 [256, 512], P('expert', 'mp'), may hold values from -6 to 6
- cache_lengths: int32 [256], P('expert'), may hold values from 32 to 128, as said below
Outputs:
- mixed: bfloat16 [256, 4096], P('expert', 'mp')
- attended: bfloat16 [256, 2048], P('expert', 'mp')
The draws below stay inside these ranges and needn't reach their ends.
Inputs may be any that keep to these rules, and one draw needn't show every extreme that they name: `expert_ids`: in each aligned block of 16 tokens (the tokens of one index of expert) no expert is named more than 2 times, a bound that some block reaches. `cache_lengths`: some sequence has all 128 positions filled.
All inputs are finite; a program needn't handle non-finite values.
Results may differ from the reference program's by a relative error of at most 0.0055.
Values may be sent and summed in bfloat16 or wider, within the bound.
A program may use at most 128 MiB of HBM per device.

```python
import math
import jax
import jax.numpy as jnp
import numpy as np
from jax import lax

D = 4096
FF = 2048
HEAD = 128
Q_HEADS = 16
KV_HEADS = 4
CAP = 2
CTX = 128
EXPERTS = 16
TOK_DEV = 16
TOKENS = 256
N_EXPERT = 16


def draw_tokens(key, part):
    base_key = jax.random.fold_in(key, 11)
    first, second, third = jax.random.split(base_key, 3)
    row_scale = jnp.exp(jax.random.uniform(first, (TOKENS, 1), jnp.float32, math.log(0.5), math.log(2.0)))
    column_scale = jnp.exp(jax.random.uniform(second, (1, D), jnp.float32, math.log(0.3), math.log(3.0)))
    entries = jax.random.normal(third, (TOKENS, D), jnp.float32)
    return jnp.clip(entries * row_scale * column_scale, -8.0, 8.0).astype(jnp.bfloat16)


def query_key_pair(key):
    base_key = jax.random.fold_in(key, 23)
    first, second = jax.random.split(base_key, 2)
    query_draw = jnp.clip(jax.random.normal(first, (TOKENS, Q_HEADS * HEAD), jnp.float32), -4.5, 4.5)
    key_draw = jnp.clip(jax.random.normal(second, (TOKENS, CTX, KV_HEADS * HEAD), jnp.float32), -4.5, 4.5)
    return (query_draw, key_draw)


def draw_queries(key, part):
    return query_key_pair(key)[0].astype(jnp.bfloat16)


def draw_keys(key, part):
    return query_key_pair(key)[1].astype(jnp.bfloat16)


def draw_cache_lengths(key, part):
    base_key = jax.random.fold_in(key, 37)
    first, second = jax.random.split(base_key, 2)
    lengths = jax.random.randint(first, (TOKENS,), max(CTX // 4, 2), CTX + 1, jnp.int32)
    chosen = jax.random.randint(second, (), 0, TOKENS, jnp.int32)
    return jnp.where(jnp.arange(TOKENS, dtype=jnp.int32) == chosen, CTX, lengths).astype(jnp.int32)


def block_scale(key, extent, cuts, least, top_value):
    level, own = 1.0, jax.random.fold_in(key, 6)
    for position, shards_of in cuts:
        steps = jnp.exp(jax.random.uniform(jax.random.fold_in(own, position), (shards_of,), jnp.float32, least / len(cuts), top_value / len(cuts)))
        level = level * jnp.repeat(steps, extent[position] // shards_of).reshape([-1 if axis == position else 1 for axis in range(len(extent))])
    return level


def deal_out(rng, own, number, rows, count, top, most, slope):
    order = jax.random.permutation(rng, count)
    heavy_load, usual = load_shares(count, rows * top, most, slope, True), load_shares(count, rows * top, most, slope, False)
    places = jnp.arange(count)

    def named(tallies, turn):
        used = int((tallies > 0).sum())
        fixed = max(1, used // 4)
        moved = fixed + (places - fixed + turn * (used - fixed)) % max(1, count - fixed)
        return jnp.zeros((count,), jnp.int32).at[order[jnp.where(places < fixed, places, moved)]].set(jnp.asarray(tallies, jnp.int32))

    tallies = jnp.where(number % 4 == 0, named(heavy_load, number // 4), named(usual, number - number // 4 - 1))
    mixed = jax.random.permutation(jax.random.fold_in(own, 3), count)
    donor, taker = mixed[0:count // 2 * 2:2], mixed[1:count // 2 * 2:2]
    slack = jnp.minimum(tallies[donor] - 1, most - tallies[taker]) // 2
    slack = jnp.where((donor == order[0]) | (taker == order[0]) | (tallies[taker] == 0), 0, jnp.maximum(slack, 0))
    moved = jax.random.randint(jax.random.fold_in(own, 4), (count // 2,), 0, 1 << 20) % (slack + 1)
    tallies = tallies.at[donor].add(-moved).at[taker].add(moved)
    labels = jnp.searchsorted(jnp.cumsum(tallies), jnp.arange(rows * top), side="right").astype(jnp.int32)
    table = labels.reshape(top, rows).T
    table = table[jax.random.permutation(jax.random.fold_in(own, 1), rows)]
    turn = jax.random.randint(jax.random.fold_in(own, 2), (rows, 1), 0, top)
    return jnp.take_along_axis(table, (jnp.arange(top)[None, :] + turn) % top, axis=1)


def load_shares(amount, total, reach, slope, full):
    weights = [(1 << 20) // math.isqrt(standing ** slope) + 1 for standing in range(1, amount + 1)]
    largest = reach if full else min(reach, max(-(-total // amount), total * weights[0] // sum(weights)))
    least = 1 if total - largest >= amount - 1 else 0
    counts, rest = [largest] + [least] * (amount - 1), total - largest - least * (amount - 1)
    while rest > 0:
        free = [i for i in range(1, amount) if counts[i] < largest] or [i for i in range(1, amount) if counts[i] < reach]
        pool, budget = sum([weights[i] for i in free]), rest
        for i in free:
            more = min(reach - counts[i], max(1, budget * weights[i] // pool), rest)
            counts[i] = counts[i] + more
            rest = rest - more
    return np.array(counts)


def noise(rng, dims, deviation, most, pieces=(), kind=jnp.bfloat16):
    drawn = jax.random.normal(rng, dims, jnp.float32) * deviation
    if len(pieces) > 0:
        drawn = block_scale(rng, dims, pieces, -0.22, 0.18) * drawn
    return jnp.clip(drawn, min=-most, max=most).astype(kind)


def setup_inputs(seed: int = 0) -> dict:
    key_list = jax.random.split(jax.random.key(seed), 12)
    tokens = draw_tokens(jax.random.fold_in(key_list[11], 71), 0)
    norm_gain = jnp.clip(1.0 + 0.15 * jax.random.normal(key_list[1], (D,), jnp.float32), 0.25, 1.75).astype(jnp.bfloat16)
    expert_ids_keys = jax.random.split(jax.random.fold_in(key_list[2], 1), TOKENS // TOK_DEV)
    expert_ids_turns = jax.random.permutation(jax.random.fold_in(key_list[2], 3), TOKENS // TOK_DEV)
    expert_ids = jax.vmap(lambda own, number: deal_out(jax.random.fold_in(key_list[2], 2), own, number, TOK_DEV, EXPERTS, 1, CAP, 2))(expert_ids_keys, expert_ids_turns).reshape((TOKENS, 1))
    w_in = noise(key_list[3], (EXPERTS, D, FF), D ** -0.5, 0.09375, ((0, 16), (2, 2)))
    w_out = noise(key_list[4], (EXPERTS, FF, D), FF ** -0.5, 0.125, ((0, 16), (1, 2)))
    queries = draw_queries(jax.random.fold_in(key_list[11], 71), 0)
    keys = draw_keys(jax.random.fold_in(key_list[11], 71), 0)
    values = noise(key_list[7], (TOKENS, CTX, KV_HEADS * HEAD), 1.0, 6.0, ((0, 16), (2, 2)))
    new_keys = noise(key_list[8], (TOKENS, KV_HEADS * HEAD), 1.5, 9.0, ((0, 16), (1, 2)))
    new_values = noise(key_list[9], (TOKENS, KV_HEADS * HEAD), 1.0, 6.0, ((0, 16), (1, 2)))
    cache_lengths = draw_cache_lengths(jax.random.fold_in(key_list[11], 71), 0)
    return {"tokens": tokens, "norm_gain": norm_gain, "expert_ids": expert_ids, "w_in": w_in, "w_out": w_out, "queries": queries, "keys": keys, "values": values, "new_keys": new_keys, "new_values": new_values, "cache_lengths": cache_lengths}


def expert_apply(expert_item):
    arrived, first, second = expert_item
    hidden = jnp.maximum(jnp.dot(arrived, first, preferred_element_type=jnp.float32), 0.0).astype(jnp.bfloat16)
    return jnp.dot(hidden, second, preferred_element_type=jnp.float32).astype(jnp.bfloat16)

def attend_block(block_item):
    query_part, key_part, value_part, newkey_part, newvalue_part, length_part = block_item
    seq_count = query_part.shape[0]
    group_size = Q_HEADS // KV_HEADS
    score_scale = HEAD ** (-0.5)
    query_heads = query_part.astype(jnp.float32).reshape(seq_count, KV_HEADS, group_size, HEAD)
    key_heads = key_part.astype(jnp.float32).reshape(seq_count, CTX, KV_HEADS, HEAD)
    value_heads = value_part.astype(jnp.float32).reshape(seq_count, CTX, KV_HEADS, HEAD)
    newkey_heads = newkey_part.astype(jnp.float32).reshape(seq_count, KV_HEADS, HEAD)
    newvalue_heads = newvalue_part.astype(jnp.float32).reshape(seq_count, KV_HEADS, 1, HEAD)
    scores = jnp.einsum('skgd,sckd->skgc', query_heads, key_heads) * score_scale
    own_score = jnp.einsum('skgd,skd->skg', query_heads, newkey_heads) * score_scale
    visible = (jnp.arange(CTX, dtype=jnp.int32)[None, :] < length_part[:, None])[:, None, None, :]
    scores = jnp.where(visible, scores, -1e+30)
    highest = jnp.maximum(lax.optimization_barrier(jnp.max(scores, axis=-1)), own_score)
    cache_terms = jnp.exp(scores - highest[..., None])
    own_term = jnp.exp(own_score - highest)
    denominator = lax.optimization_barrier(jnp.sum(cache_terms, axis=-1)) + own_term
    weights = (cache_terms / denominator[..., None]).astype(jnp.bfloat16)
    own_weight = (own_term / denominator).astype(jnp.bfloat16)
    output = jnp.einsum('skgc,sckd->skgd', weights.astype(jnp.float32), value_heads)
    output = output + own_weight.astype(jnp.float32)[..., None] * newvalue_heads
    return output.reshape(seq_count, Q_HEADS * HEAD).astype(jnp.bfloat16)

def reference(tokens, norm_gain, expert_ids, w_in, w_out, queries, keys, values, new_keys, new_values, cache_lengths):
    residual = tokens.astype(jnp.float32)
    mean_square = lax.optimization_barrier(jnp.mean(residual * residual, axis=-1, keepdims=True))
    normed = (residual * lax.rsqrt(mean_square + 1e-05) * norm_gain.astype(jnp.float32)[None, :]).astype(jnp.bfloat16)
    expert_row = expert_ids[:, 0].astype(jnp.int32)
    expert_count = w_in.shape[0]
    onehot = (expert_row[:, None] == jnp.arange(expert_count, dtype=jnp.int32)[None, :]).astype(jnp.int32)
    blocked = onehot.reshape(-1, TOK_DEV, expert_count)
    earlier = (jnp.cumsum(blocked, axis=1) - blocked).reshape(-1, expert_count)
    slot_index = lax.optimization_barrier(jnp.sum(earlier * onehot, axis=1)).astype(jnp.int32)
    source = (jnp.arange(expert_row.shape[0], dtype=jnp.int32) // TOK_DEV).astype(jnp.int32)
    target = (source * CAP + slot_index).astype(jnp.int32)
    buffer = jnp.zeros((expert_count, N_EXPERT * CAP, D), jnp.bfloat16).at[expert_row, target].set(normed)
    results = lax.map(expert_apply, (buffer, w_in, w_out))
    expert_out = results[expert_row, target]
    mixed = (residual + expert_out.astype(jnp.float32)).astype(jnp.bfloat16)
    block_count = queries.shape[0] // TOK_DEV
    attended = lax.map(attend_block, (queries.reshape(block_count, TOK_DEV, Q_HEADS * HEAD), keys.reshape(block_count, TOK_DEV, CTX, KV_HEADS * HEAD), values.reshape(block_count, TOK_DEV, CTX, KV_HEADS * HEAD), new_keys.reshape(block_count, TOK_DEV, KV_HEADS * HEAD), new_values.reshape(block_count, TOK_DEV, KV_HEADS * HEAD), cache_lengths.reshape(block_count, TOK_DEV)))
    attended = attended.reshape(-1, Q_HEADS * HEAD)
    return (mixed, attended)
```

```python
import functools

import jax
import jax.numpy as jnp
from jax import lax
from jax.experimental import pallas as pl
from jax.experimental.pallas import tpu as pltpu
from jax.sharding import PartitionSpec as P

HEAD = 128
CAP = 2
RETURN_PIECES = 2
F32 = jnp.float32
BF16 = jnp.bfloat16
MESH = pl.DeviceIdType.MESH


def step_kernel(
    experts,
    lens,
    tok_h,
    gain_h,
    ids_h,
    win_h,
    wout_h,
    q_h,
    k_h,
    v_h,
    nk_h,
    nv_h,
    mixed,
    att,
    tok,
    gain,
    ids,
    win,
    wout,
    q,
    k,
    v,
    nk,
    nv,
    out2d,
    outgoing,
    arrived,
    relayed,
    x_own,
    x_other,
    hidden_part,
    part_send,
    part_recv,
    ret2d,
    ret,
    back,
    back2d,
    q_rows,
    nk_rows,
    nv_rows,
    score_rows,
    own_rows,
    att_rows,
    load_sem,
    send_sem,
    recv_sem,
    relay_send,
    relay_recv,
    part_ssem,
    part_rsem,
    ret_send,
    ret_recv,
):
    rows, width = tok.shape
    half = width // 2
    me = lax.axis_index("expert")
    core = lax.axis_index("mp")
    other = 1 - core
    own_off = pl.multiple_of(core * half, half)
    other_off = pl.multiple_of(other * half, half)
    slots = experts * CAP

    loads = [
        pltpu.make_async_copy(src, dst, load_sem.at[n])
        for n, (src, dst) in enumerate(
            [
                (tok_h, tok),
                (ids_h, ids),
                (gain_h, gain),
                (q_h, q),
                (nk_h, nk),
                (nv_h, nv),
                (k_h, k),
                (v_h, v),
                (win_h.at[0, pl.ds(own_off, half), :], win.at[0]),
                (win_h.at[0, pl.ds(other_off, half), :], win.at[1]),
                (wout_h.at[0, :, pl.ds(other_off, half)], wout.at[0]),
                (wout_h.at[0, :, pl.ds(own_off, half)], wout.at[1]),
            ]
        )
    ]
    for load in loads[:3]:
        load.start()

    barrier = pltpu.get_barrier_semaphore()
    for i in range(1, experts):
        pl.semaphore_signal(
            barrier, inc=1, device_id=(lax.rem(me + i, experts), core), device_id_type=MESH
        )
    pl.semaphore_signal(barrier, inc=1, device_id=(me, other), device_id_type=MESH)
    for load in loads[3:]:
        load.start()

    for load in loads[:3]:
        load.wait()
    whole = tok[...].astype(F32)
    inverse = lax.rsqrt(jnp.mean(whole * whole, axis=-1, keepdims=True) + 1e-05)
    mine = tok[:, pl.ds(own_off, half)].astype(F32)
    normed = (mine * inverse * gain[:, pl.ds(own_off, half)].astype(F32)).astype(BF16)
    relative = ids[...] - me
    relative = jnp.where(relative < 0, relative + experts, relative)
    onehot = relative == lax.broadcasted_iota(jnp.int32, (rows, experts), 1)
    onehot = jnp.where(onehot, 1.0, 0.0)
    r_i = lax.broadcasted_iota(jnp.int32, (rows, rows), 0)
    c_i = lax.broadcasted_iota(jnp.int32, (rows, rows), 1)
    below = jnp.where(c_i < r_i, 1.0, 0.0).astype(BF16)
    earlier = jnp.dot(below, onehot.astype(BF16), preferred_element_type=F32)
    slot = jnp.sum(earlier * onehot, axis=1, keepdims=True)
    target = relative.astype(F32) * CAP + slot
    placed_t = jnp.where(
        target == lax.broadcasted_iota(jnp.int32, (rows, slots), 1).astype(F32), 1.0, 0.0
    ).astype(BF16)
    spread = jnp.where(r_i == c_i, target, 0.0).astype(BF16)
    target_rows = jnp.dot(jnp.ones((slots, rows), BF16), spread, preferred_element_type=F32)
    placed = jnp.where(
        target_rows == lax.broadcasted_iota(jnp.int32, (slots, rows), 0).astype(F32), 1.0, 0.0
    ).astype(BF16)
    out2d[...] = jnp.dot(placed, normed, preferred_element_type=F32).astype(BF16)
    for i in range(experts):
        outgoing[i] = out2d[CAP * i : CAP * (i + 1), :]

    pl.semaphore_wait(barrier, experts)

    def relay(i):
        return pltpu.make_async_remote_copy(
            src_ref=outgoing.at[0] if i == 0 else arrived.at[i],
            dst_ref=relayed.at[i],
            send_sem=relay_send.at[i],
            recv_sem=relay_recv.at[i],
            device_id=(me, other),
            device_id_type=MESH,
        )

    def send(i):
        return pltpu.make_async_remote_copy(
            src_ref=outgoing.at[i],
            dst_ref=arrived.at[i],
            send_sem=send_sem.at[i],
            recv_sem=recv_sem.at[i],
            device_id=(lax.rem(me + i, experts), core),
            device_id_type=MESH,
        )

    for i in range(1, experts):
        send(i).start()
    relay(0).start()
    x_own[0:CAP, :] = out2d[0:CAP, :]

    kv_heads = nk.shape[1] // HEAD
    heads = q.shape[1] // HEAD
    group = heads // kv_heads
    ctx = k.shape[1]
    for load in loads[3:7]:
        load.wait()
    for h in range(heads):
        q_rows[h * rows : (h + 1) * rows, :] = q[:, h * HEAD : (h + 1) * HEAD].astype(F32)
    nk_rows[...] = nk[...].astype(F32)
    nv_rows[...] = nv[...].astype(F32)
    lane = lax.broadcasted_iota(jnp.int32, (heads, ctx), 1)
    head_of = lax.broadcasted_iota(jnp.int32, (heads, HEAD), 0) // group
    scale = HEAD ** (-0.5)

    def attend_scores(lo, hi):
        for s in range(lo, hi):
            q_s = q_rows[pl.ds(s, heads, stride=rows), :]
            wide = jnp.concatenate(
                [jnp.where(head_of == j, q_s, 0.0) for j in range(kv_heads)], axis=1
            )
            scores = lax.dot_general(
                wide.astype(BF16), k[s], (((1,), (1,)), ((), ())), preferred_element_type=F32
            )
            own = jnp.sum(wide * nk_rows[s : s + 1, :], axis=1, keepdims=True)
            score_rows[s * heads : (s + 1) * heads, :] = jnp.where(
                lane < lens[s], scores * scale, -1e30
            )
            own_rows[s * heads : (s + 1) * heads, :] = own * scale

    def attend_values(lo, hi):
        part = slice(lo * heads, hi * heads)
        scores = score_rows[part, :]
        own = own_rows[part, :]
        highest = jnp.maximum(jnp.max(scores, axis=1, keepdims=True), own)
        terms = jnp.exp(scores - highest)
        own_term = jnp.exp(own - highest)
        total = jnp.sum(terms, axis=1, keepdims=True) + own_term
        weights = (terms / total).astype(BF16)
        own_weight = (own_term / total).astype(BF16).astype(F32)
        for s in range(lo, hi):
            at = (s - lo) * heads
            full = jnp.dot(weights[at : at + heads, :], v[s], preferred_element_type=F32)
            full = full + own_weight[at : at + heads, :] * nv_rows[s : s + 1, :]
            picked = full[:, 0:HEAD]
            for j in range(1, kv_heads):
                picked = jnp.where(head_of == j, full[:, j * HEAD : (j + 1) * HEAD], picked)
            att_rows[pl.ds(s, heads, stride=rows), :] = picked

    attend_scores(0, rows)

    for i in range(1, experts):
        send(i).wait_recv()
        relay(i).start()
        x_own[CAP * i : CAP * (i + 1), :] = arrived[i]
    loads[8].wait()
    hidden_part[...] = jnp.dot(x_own[...], win[0], preferred_element_type=F32)
    for i in range(experts):
        relay(i).wait_recv()
        x_other[CAP * i : CAP * (i + 1), :] = relayed[i]
    loads[9].wait()
    hidden = jnp.maximum(
        hidden_part[...] + jnp.dot(x_other[...], win[1], preferred_element_type=F32), 0.0
    ).astype(BF16)

    piece = half // RETURN_PIECES

    def part_copy(c):
        return pltpu.make_async_remote_copy(
            src_ref=part_send.at[c],
            dst_ref=part_recv.at[c],
            send_sem=part_ssem.at[c],
            recv_sem=part_rsem.at[c],
            device_id=(me, other),
            device_id_type=MESH,
        )

    def give_back(c, i):
        return pltpu.make_async_remote_copy(
            src_ref=ret.at[c, i],
            dst_ref=back.at[c, i],
            send_sem=ret_send.at[c, i],
            recv_sem=ret_recv.at[c, i],
            device_id=(lax.rem(me + experts - i, experts), core),
            device_id_type=MESH,
        )

    loads[10].wait()
    for c in range(RETURN_PIECES):
        part_send[c] = jnp.dot(
            hidden, wout[0, :, c * piece : (c + 1) * piece], preferred_element_type=F32
        ).astype(BF16)
        part_copy(c).start()
    loads[11].wait()
    for c in range(RETURN_PIECES):
        cols = slice(c * piece, (c + 1) * piece)
        own_part = jnp.dot(hidden, wout[1, :, cols], preferred_element_type=F32)
        part_copy(c).wait_recv()
        ret2d[c] = (own_part + part_recv[c].astype(F32)).astype(BF16)
        for i in range(1, experts):
            ret[c, i] = ret2d[c, CAP * i : CAP * (i + 1), :]
            give_back(c, i).start()
        back2d[0:CAP, cols] = ret2d[c, 0:CAP, :]

    loads[7].wait()
    attend_values(0, rows)
    for h in range(heads):
        att[:, h * HEAD : (h + 1) * HEAD] = att_rows[h * rows : (h + 1) * rows, :].astype(BF16)

    for c in range(RETURN_PIECES):
        cols = slice(c * piece, (c + 1) * piece)
        for i in range(1, experts):
            give_back(c, i).wait_recv()
            back2d[CAP * i : CAP * (i + 1), cols] = back[c, i]
        expert_out = jnp.dot(placed_t, back2d[:, cols], preferred_element_type=F32)
        at = pl.multiple_of(own_off + c * piece, piece)
        mixed[:, cols] = (tok[:, pl.ds(at, piece)].astype(F32) + expert_out).astype(BF16)

    for i in range(1, experts):
        send(i).wait_send()
    for i in range(experts):
        relay(i).wait_send()
    for c in range(RETURN_PIECES):
        part_copy(c).wait_send()
        for i in range(1, experts):
            give_back(c, i).wait_send()


def shards(tokens, norm_gain, expert_ids, w_in, w_out, queries, keys, values, new_keys, new_values, lens):
    experts = lax.axis_size("expert")
    rows, width = tokens.shape
    half = width // 2
    inner = w_in.shape[2]
    slots = experts * CAP
    heads = queries.shape[1] // HEAD
    ctx = keys.shape[1]
    piece = half // RETURN_PIECES
    dma = pltpu.SemaphoreType.DMA
    gain = norm_gain.reshape(1, width)
    any_spec = pl.BlockSpec(memory_space=pl.ANY)
    vmem = pl.BlockSpec(memory_space=pltpu.VMEM)
    like = lambda a: pltpu.VMEM(a.shape, a.dtype)
    return pl.pallas_call(
        functools.partial(step_kernel, experts),
        out_shape=(
            jax.ShapeDtypeStruct((rows, half), BF16),
            jax.ShapeDtypeStruct(queries.shape, BF16),
        ),
        in_specs=[pl.BlockSpec(memory_space=pltpu.SMEM)] + [any_spec] * 10,
        out_specs=(vmem, vmem),
        scratch_shapes=[
            like(tokens),
            like(gain),
            like(expert_ids),
            pltpu.VMEM((2, half, inner), BF16),
            pltpu.VMEM((2, inner, half), BF16),
            like(queries),
            like(keys),
            like(values),
            like(new_keys),
            like(new_values),
            pltpu.VMEM((slots, half), BF16),
            pltpu.VMEM((experts, CAP, half), BF16),
            pltpu.VMEM((experts, CAP, half), BF16),
            pltpu.VMEM((experts, CAP, half), BF16),
            pltpu.VMEM((slots, half), BF16),
            pltpu.VMEM((slots, half), BF16),
            pltpu.VMEM((slots, inner), F32),
            pltpu.VMEM((RETURN_PIECES, slots, piece), BF16),
            pltpu.VMEM((RETURN_PIECES, slots, piece), BF16),
            pltpu.VMEM((RETURN_PIECES, slots, piece), BF16),
            pltpu.VMEM((RETURN_PIECES, experts, CAP, piece), BF16),
            pltpu.VMEM((RETURN_PIECES, experts, CAP, piece), BF16),
            pltpu.VMEM((slots, half), BF16),
            pltpu.VMEM((heads * rows, HEAD), F32),
            pltpu.VMEM(new_keys.shape, F32),
            pltpu.VMEM(new_values.shape, F32),
            pltpu.VMEM((heads * rows, ctx), F32),
            pltpu.VMEM((heads * rows, 1), F32),
            pltpu.VMEM((heads * rows, HEAD), F32),
            dma((12,)),
            dma((experts,)),
            dma((experts,)),
            dma((experts,)),
            dma((experts,)),
            dma((RETURN_PIECES,)),
            dma((RETURN_PIECES,)),
            dma((RETURN_PIECES, experts)),
            dma((RETURN_PIECES, experts)),
        ],
        compiler_params=pltpu.CompilerParams(
            collective_id=0, has_side_effects=True, vmem_limit_bytes=60 * 1024 * 1024
        ),
    )(lens, tokens, gain, expert_ids, w_in, w_out, queries, keys, values, new_keys, new_values)


def solution(mesh):
    return jax.shard_map(
        shards,
        mesh=mesh,
        in_specs=(
            P("expert", None),
            P(),
            P("expert", None),
            P("expert", None, "mp"),
            P("expert", "mp", None),
            P("expert", "mp"),
            P("expert", None, "mp"),
            P("expert", None, "mp"),
            P("expert", "mp"),
            P("expert", "mp"),
            P("expert"),
        ),
        out_specs=(P("expert", "mp"), P("expert", "mp")),
        check_vma=False,
    )
```

```python
import functools

import jax
import jax.numpy as jnp
from jax import lax
from jax.experimental import pallas as pl
from jax.experimental.pallas import tpu as pltpu
from jax.sharding import PartitionSpec as P

HEAD = 128
CAP = 2
RETURN_PIECES = 2
F32 = jnp.float32
BF16 = jnp.bfloat16
MESH = pl.DeviceIdType.MESH


def step_kernel(
    experts,
    lens,
    tok_h,
    gain_h,
    ids_h,
    win_h,
    wout_h,
    q_h,
    k_h,
    v_h,
    nk_h,
    nv_h,
    mixed,
    att,
    tok,
    gain,
    ids,
    win,
    wout,
    q,
    k,
    v,
    nk,
    nv,
    out2d,
    outgoing,
    arrived,
    relayed,
    x_own,
    x_other,
    hidden_part,
    part_send,
    part_recv,
    ret2d,
    ret,
    back,
    back2d,
    q_rows,
    nk_rows,
    nv_rows,
    score_rows,
    own_rows,
    att_rows,
    load_sem,
    send_sem,
    recv_sem,
    relay_send,
    relay_recv,
    part_ssem,
    part_rsem,
    ret_send,
    ret_recv,
):
    rows, width = tok.shape
    half = width // 2
    me = lax.axis_index("expert")
    core = lax.axis_index("mp")
    other = 1 - core
    own_off = pl.multiple_of(core * half, half)
    other_off = pl.multiple_of(other * half, half)
    slots = experts * CAP

    loads = [
        pltpu.make_async_copy(src, dst, load_sem.at[n])
        for n, (src, dst) in enumerate(
            [
                (tok_h, tok),
                (ids_h, ids),
                (gain_h, gain),
                (q_h, q),
                (nk_h, nk),
                (nv_h, nv),
                (k_h, k),
                (v_h, v),
                (win_h.at[0, pl.ds(own_off, half), :], win.at[0]),
                (win_h.at[0, pl.ds(other_off, half), :], win.at[1]),
                (wout_h.at[0, :, pl.ds(other_off, half)], wout.at[0]),
                (wout_h.at[0, :, pl.ds(own_off, half)], wout.at[1]),
            ]
        )
    ]
    for load in loads[:3]:
        load.start()

    barrier = pltpu.get_barrier_semaphore()
    for i in range(1, experts):
        pl.semaphore_signal(
            barrier, inc=1, device_id=(lax.rem(me + i, experts), core), device_id_type=MESH
        )
    pl.semaphore_signal(barrier, inc=1, device_id=(me, other), device_id_type=MESH)
    for load in loads[3:]:
        load.start()

    for load in loads[:3]:
        load.wait()
    whole = tok[...].astype(F32)
    inverse = lax.rsqrt(jnp.mean(whole * whole, axis=-1, keepdims=True) + 1e-05)
    mine = tok[:, pl.ds(own_off, half)].astype(F32)
    normed = (mine * inverse * gain[pl.ds(own_off, half)].astype(F32)[None, :]).astype(BF16)
    relative = ids[...] - me
    relative = jnp.where(relative < 0, relative + experts, relative)
    onehot = relative == lax.broadcasted_iota(jnp.int32, (experts, rows), 0)
    onehot = jnp.where(onehot, 1.0, 0.0)
    r_i = lax.broadcasted_iota(jnp.int32, (rows, rows), 0)
    c_i = lax.broadcasted_iota(jnp.int32, (rows, rows), 1)
    above = jnp.where(r_i < c_i, 1.0, 0.0).astype(BF16)
    earlier = jnp.dot(onehot.astype(BF16), above, preferred_element_type=F32)
    slot = jnp.sum(earlier * onehot, axis=0, keepdims=True)
    target = relative.astype(F32) * CAP + slot
    placed = jnp.where(
        target == lax.broadcasted_iota(jnp.int32, (slots, rows), 0).astype(F32), 1.0, 0.0
    ).astype(BF16)
    spread = jnp.where(r_i == c_i, target, 0.0).astype(BF16)
    target_cols = jnp.dot(spread, jnp.ones((rows, slots), BF16), preferred_element_type=F32)
    placed_t = jnp.where(
        target_cols == lax.broadcasted_iota(jnp.int32, (rows, slots), 1).astype(F32), 1.0, 0.0
    ).astype(BF16)
    out2d[...] = jnp.dot(placed, normed, preferred_element_type=F32).astype(BF16)
    for i in range(experts):
        outgoing[i] = out2d[CAP * i : CAP * (i + 1), :]

    pl.semaphore_wait(barrier, experts)

    def relay(i):
        return pltpu.make_async_remote_copy(
            src_ref=outgoing.at[0] if i == 0 else arrived.at[i],
            dst_ref=relayed.at[i],
            send_sem=relay_send.at[i],
            recv_sem=relay_recv.at[i],
            device_id=(me, other),
            device_id_type=MESH,
        )

    def send(i):
        return pltpu.make_async_remote_copy(
            src_ref=outgoing.at[i],
            dst_ref=arrived.at[i],
            send_sem=send_sem.at[i],
            recv_sem=recv_sem.at[i],
            device_id=(lax.rem(me + i, experts), core),
            device_id_type=MESH,
        )

    for i in range(1, experts):
        send(i).start()
    relay(0).start()
    x_own[0:CAP, :] = out2d[0:CAP, :]

    kv_heads = nk.shape[1] // HEAD
    heads = q.shape[1] // HEAD
    group = heads // kv_heads
    ctx = k.shape[1]
    for load in loads[3:7]:
        load.wait()
    for h in range(heads):
        q_rows[h * rows : (h + 1) * rows, :] = q[:, h * HEAD : (h + 1) * HEAD].astype(F32)
    nk_rows[...] = nk[...].astype(F32)
    nv_rows[...] = nv[...].astype(F32)
    lane = lax.broadcasted_iota(jnp.int32, (heads, ctx), 1)
    head_of = lax.broadcasted_iota(jnp.int32, (heads, HEAD), 0) // group
    scale = HEAD ** (-0.5)

    def attend_scores(lo, hi):
        for s in range(lo, hi):
            q_s = q_rows[pl.ds(s, heads, stride=rows), :]
            wide = jnp.concatenate(
                [jnp.where(head_of == j, q_s, 0.0) for j in range(kv_heads)], axis=1
            )
            scores = lax.dot_general(
                wide.astype(BF16), k[s], (((1,), (1,)), ((), ())), preferred_element_type=F32
            )
            own = jnp.sum(wide * nk_rows[s : s + 1, :], axis=1, keepdims=True)
            score_rows[s * heads : (s + 1) * heads, :] = jnp.where(
                lane < lens[s], scores * scale, -1e30
            )
            own_rows[s * heads : (s + 1) * heads, :] = own * scale

    def attend_values(lo, hi):
        part = slice(lo * heads, hi * heads)
        scores = score_rows[part, :]
        own = own_rows[part, :]
        highest = jnp.maximum(jnp.max(scores, axis=1, keepdims=True), own)
        terms = jnp.exp(scores - highest)
        own_term = jnp.exp(own - highest)
        total = jnp.sum(terms, axis=1, keepdims=True) + own_term
        weights = (terms / total).astype(BF16)
        own_weight = (own_term / total).astype(BF16).astype(F32)
        for s in range(lo, hi):
            at = (s - lo) * heads
            full = jnp.dot(weights[at : at + heads, :], v[s], preferred_element_type=F32)
            full = full + own_weight[at : at + heads, :] * nv_rows[s : s + 1, :]
            picked = full[:, 0:HEAD]
            for j in range(1, kv_heads):
                picked = jnp.where(head_of == j, full[:, j * HEAD : (j + 1) * HEAD], picked)
            att_rows[pl.ds(s, heads, stride=rows), :] = picked

    attend_scores(0, rows)

    for i in range(1, experts):
        send(i).wait_recv()
        relay(i).start()
        x_own[CAP * i : CAP * (i + 1), :] = arrived[i]
    loads[8].wait()
    hidden_part[...] = jnp.dot(x_own[...], win[0], preferred_element_type=F32)
    for i in range(experts):
        relay(i).wait_recv()
        x_other[CAP * i : CAP * (i + 1), :] = relayed[i]
    loads[9].wait()
    hidden = jnp.maximum(
        hidden_part[...] + jnp.dot(x_other[...], win[1], preferred_element_type=F32), 0.0
    ).astype(BF16)

    piece = half // RETURN_PIECES

    def part_copy(c):
        return pltpu.make_async_remote_copy(
            src_ref=part_send.at[c],
            dst_ref=part_recv.at[c],
            send_sem=part_ssem.at[c],
            recv_sem=part_rsem.at[c],
            device_id=(me, other),
            device_id_type=MESH,
        )

    def give_back(c, i):
        return pltpu.make_async_remote_copy(
            src_ref=ret.at[c, i],
            dst_ref=back.at[c, i],
            send_sem=ret_send.at[c, i],
            recv_sem=ret_recv.at[c, i],
            device_id=(lax.rem(me + experts - i, experts), core),
            device_id_type=MESH,
        )

    loads[10].wait()
    for c in range(RETURN_PIECES):
        part_send[c] = jnp.dot(
            hidden, wout[0, :, c * piece : (c + 1) * piece], preferred_element_type=F32
        ).astype(BF16)
        part_copy(c).start()
    loads[11].wait()
    for c in range(RETURN_PIECES):
        cols = slice(c * piece, (c + 1) * piece)
        own_part = jnp.dot(hidden, wout[1, :, cols], preferred_element_type=F32)
        part_copy(c).wait_recv()
        ret2d[c] = (own_part + part_recv[c].astype(F32)).astype(BF16)
        for i in range(1, experts):
            ret[c, i] = ret2d[c, CAP * i : CAP * (i + 1), :]
            give_back(c, i).start()
        back2d[0:CAP, cols] = ret2d[c, 0:CAP, :]

    loads[7].wait()
    attend_values(0, rows)
    for h in range(heads):
        att[:, h * HEAD : (h + 1) * HEAD] = att_rows[h * rows : (h + 1) * rows, :].astype(BF16)

    for c in range(RETURN_PIECES):
        cols = slice(c * piece, (c + 1) * piece)
        for i in range(1, experts):
            give_back(c, i).wait_recv()
            back2d[CAP * i : CAP * (i + 1), cols] = back[c, i]
        expert_out = jnp.dot(placed_t, back2d[:, cols], preferred_element_type=F32)
        at = pl.multiple_of(own_off + c * piece, piece)
        mixed[:, cols] = (tok[:, pl.ds(at, piece)].astype(F32) + expert_out).astype(BF16)

    for i in range(1, experts):
        send(i).wait_send()
    for i in range(experts):
        relay(i).wait_send()
    for c in range(RETURN_PIECES):
        part_copy(c).wait_send()
        for i in range(1, experts):
            give_back(c, i).wait_send()


def finish_kernel(mixed_in, att_in, mixed, att, sem):
    copies = [
        pltpu.make_async_copy(mixed_in, mixed, sem.at[0]),
        pltpu.make_async_copy(att_in, att, sem.at[1]),
    ]
    for copy in copies:
        copy.start()
    for copy in copies:
        copy.wait()


def shards(tokens, norm_gain, expert_ids, w_in, w_out, queries, keys, values, new_keys, new_values, lens):
    experts = lax.axis_size("expert")
    rows, width = tokens.shape
    half = width // 2
    inner = w_in.shape[2]
    slots = experts * CAP
    heads = queries.shape[1] // HEAD
    ctx = keys.shape[1]
    piece = half // RETURN_PIECES
    dma = pltpu.SemaphoreType.DMA
    ids = expert_ids.reshape(1, rows)
    hbm = pl.BlockSpec(memory_space=pltpu.HBM)
    vmem = pl.BlockSpec(memory_space=pltpu.VMEM)
    like = lambda a: pltpu.VMEM(a.shape, a.dtype)
    outs = (
            jax.ShapeDtypeStruct((rows, half), BF16),
            jax.ShapeDtypeStruct(queries.shape, BF16),
        )
    mixed, att = pl.pallas_call(
        functools.partial(step_kernel, experts),
        out_shape=(pltpu.VMEM((rows, half), BF16), pltpu.VMEM(queries.shape, BF16)),
        in_specs=[pl.BlockSpec(memory_space=pltpu.SMEM)] + [hbm] * 10,
        out_specs=(vmem, vmem),
        scratch_shapes=[
            like(tokens),
            like(norm_gain),
            like(ids),
            pltpu.VMEM((2, half, inner), BF16),
            pltpu.VMEM((2, inner, half), BF16),
            like(queries),
            like(keys),
            like(values),
            like(new_keys),
            like(new_values),
            pltpu.VMEM((slots, half), BF16),
            pltpu.VMEM((experts, CAP, half), BF16),
            pltpu.VMEM((experts, CAP, half), BF16),
            pltpu.VMEM((experts, CAP, half), BF16),
            pltpu.VMEM((slots, half), BF16),
            pltpu.VMEM((slots, half), BF16),
            pltpu.VMEM((slots, inner), F32),
            pltpu.VMEM((RETURN_PIECES, slots, piece), BF16),
            pltpu.VMEM((RETURN_PIECES, slots, piece), BF16),
            pltpu.VMEM((RETURN_PIECES, slots, piece), BF16),
            pltpu.VMEM((RETURN_PIECES, experts, CAP, piece), BF16),
            pltpu.VMEM((RETURN_PIECES, experts, CAP, piece), BF16),
            pltpu.VMEM((slots, half), BF16),
            pltpu.VMEM((heads * rows, HEAD), F32),
            pltpu.VMEM(new_keys.shape, F32),
            pltpu.VMEM(new_values.shape, F32),
            pltpu.VMEM((heads * rows, ctx), F32),
            pltpu.VMEM((heads * rows, 1), F32),
            pltpu.VMEM((heads * rows, HEAD), F32),
            dma((12,)),
            dma((experts,)),
            dma((experts,)),
            dma((experts,)),
            dma((experts,)),
            dma((RETURN_PIECES,)),
            dma((RETURN_PIECES,)),
            dma((RETURN_PIECES, experts)),
            dma((RETURN_PIECES, experts)),
        ],
        compiler_params=pltpu.CompilerParams(
            collective_id=0, has_side_effects=True, vmem_limit_bytes=60 * 1024 * 1024
        ),
    )(lens, tokens, norm_gain, ids, w_in, w_out, queries, keys, values, new_keys, new_values)
    return pl.pallas_call(
        finish_kernel,
        out_shape=outs,
        in_specs=[vmem, vmem],
        out_specs=(hbm, hbm),
        scratch_shapes=[dma((2,))],
        compiler_params=pltpu.CompilerParams(vmem_limit_bytes=1024 * 1024),
    )(mixed, att)


def solution(mesh):
    return jax.shard_map(
        shards,
        mesh=mesh,
        in_specs=(
            P("expert", None),
            P(),
            P("expert", None),
            P("expert", None, "mp"),
            P("expert", "mp", None),
            P("expert", "mp"),
            P("expert", None, "mp"),
            P("expert", None, "mp"),
            P("expert", "mp"),
            P("expert", "mp"),
            P("expert"),
        ),
        out_specs=(P("expert", "mp"), P("expert", "mp")),
        check_vma=False,
    )
```

```python
import functools

import jax
import jax.numpy as jnp
from jax import lax
from jax.experimental import pallas as pl
from jax.experimental.pallas import tpu as pltpu
from jax.sharding import PartitionSpec as P

HEAD = 128
CAP = 2
RETURN_PIECES = 2
F32 = jnp.float32
BF16 = jnp.bfloat16
MESH = pl.DeviceIdType.MESH


def partner(me, i):
    bit = 1
    at = me
    while bit <= i:
        if i & bit:
            at = at + bit - 2 * bit * (me // bit % 2)
        bit *= 2
    return at


def step_kernel(
    experts,
    lens,
    tok_h,
    gain_h,
    ids_h,
    win_h,
    wout_h,
    q_h,
    k_h,
    v_h,
    nk_h,
    nv_h,
    mixed,
    att,
    tok,
    gain,
    ids,
    win,
    wout,
    q,
    k,
    v,
    nk,
    nv,
    out2d,
    outgoing,
    arrived,
    relayed,
    x_own,
    x_other,
    hidden_part,
    part_send,
    part_recv,
    ret2d,
    ret,
    back,
    back2d,
    q_rows,
    nk_rows,
    nv_rows,
    score_rows,
    own_rows,
    att_rows,
    load_sem,
    send_sem,
    recv_sem,
    relay_send,
    relay_recv,
    part_ssem,
    part_rsem,
    ret_send,
    ret_recv,
):
    rows, width = tok.shape
    half = width // 2
    me = lax.axis_index("expert")
    core = lax.axis_index("mp")
    other = 1 - core
    own_off = pl.multiple_of(core * half, half)
    other_off = pl.multiple_of(other * half, half)
    slots = experts * CAP
    far_first = range(experts - 1, 0, -1)

    loads = [
        pltpu.make_async_copy(src, dst, load_sem.at[n])
        for n, (src, dst) in enumerate(
            [
                (tok_h, tok),
                (ids_h, ids),
                (gain_h, gain),
                (q_h, q),
                (nk_h, nk),
                (nv_h, nv),
                (k_h, k),
                (v_h, v),
                (win_h.at[0, pl.ds(own_off, half), :], win.at[0]),
                (win_h.at[0, pl.ds(other_off, half), :], win.at[1]),
                (wout_h.at[0, :, pl.ds(other_off, half)], wout.at[0]),
                (wout_h.at[0, :, pl.ds(own_off, half)], wout.at[1]),
            ]
        )
    ]
    for load in loads[:3]:
        load.start()

    barrier = pltpu.get_barrier_semaphore()
    for i in far_first:
        pl.semaphore_signal(
            barrier, inc=1, device_id=(partner(me, i), core), device_id_type=MESH
        )
    pl.semaphore_signal(barrier, inc=1, device_id=(me, other), device_id_type=MESH)
    for load in loads[3:]:
        load.start()

    for load in loads[:3]:
        load.wait()
    whole = tok[...].astype(F32)
    inverse = lax.rsqrt(jnp.mean(whole * whole, axis=-1, keepdims=True) + 1e-05)
    mine = tok[:, pl.ds(own_off, half)].astype(F32)
    normed = (mine * inverse * gain[pl.ds(own_off, half)].astype(F32)[None, :]).astype(BF16)
    relative = jnp.bitwise_xor(ids[...], me)
    onehot = relative == lax.broadcasted_iota(jnp.int32, (experts, rows), 0)
    onehot = jnp.where(onehot, 1.0, 0.0)
    r_i = lax.broadcasted_iota(jnp.int32, (rows, rows), 0)
    c_i = lax.broadcasted_iota(jnp.int32, (rows, rows), 1)
    above = jnp.where(r_i < c_i, 1.0, 0.0).astype(BF16)
    earlier = jnp.dot(onehot.astype(BF16), above, preferred_element_type=F32)
    slot = jnp.sum(earlier * onehot, axis=0, keepdims=True)
    target = relative.astype(F32) * CAP + slot
    placed = jnp.where(
        target == lax.broadcasted_iota(jnp.int32, (slots, rows), 0).astype(F32), 1.0, 0.0
    ).astype(BF16)
    spread = jnp.where(r_i == c_i, target, 0.0).astype(BF16)
    target_cols = jnp.dot(spread, jnp.ones((rows, slots), BF16), preferred_element_type=F32)
    placed_t = jnp.where(
        target_cols == lax.broadcasted_iota(jnp.int32, (rows, slots), 1).astype(F32), 1.0, 0.0
    ).astype(BF16)
    out2d[...] = jnp.dot(placed, normed, preferred_element_type=F32).astype(BF16)
    for i in range(experts):
        outgoing[i] = out2d[CAP * i : CAP * (i + 1), :]

    pl.semaphore_wait(barrier, experts)

    def relay(i):
        return pltpu.make_async_remote_copy(
            src_ref=outgoing.at[0] if i == 0 else arrived.at[i],
            dst_ref=relayed.at[i],
            send_sem=relay_send.at[i],
            recv_sem=relay_recv.at[i],
            device_id=(me, other),
            device_id_type=MESH,
        )

    def send(i):
        return pltpu.make_async_remote_copy(
            src_ref=outgoing.at[i],
            dst_ref=arrived.at[i],
            send_sem=send_sem.at[i],
            recv_sem=recv_sem.at[i],
            device_id=(partner(me, i), core),
            device_id_type=MESH,
        )

    for i in far_first:
        send(i).start()
    relay(0).start()
    x_own[0:CAP, :] = out2d[0:CAP, :]

    kv_heads = nk.shape[1] // HEAD
    heads = q.shape[1] // HEAD
    group = heads // kv_heads
    ctx = k.shape[1]
    for load in loads[3:7]:
        load.wait()
    for h in range(heads):
        q_rows[h * rows : (h + 1) * rows, :] = q[:, h * HEAD : (h + 1) * HEAD].astype(F32)
    nk_rows[...] = nk[...].astype(F32)
    nv_rows[...] = nv[...].astype(F32)
    lane = lax.broadcasted_iota(jnp.int32, (heads, ctx), 1)
    head_of = lax.broadcasted_iota(jnp.int32, (heads, HEAD), 0) // group
    scale = HEAD ** (-0.5)

    def attend_scores(lo, hi):
        for s in range(lo, hi):
            q_s = q_rows[pl.ds(s, heads, stride=rows), :]
            wide = jnp.concatenate(
                [jnp.where(head_of == j, q_s, 0.0) for j in range(kv_heads)], axis=1
            )
            scores = lax.dot_general(
                wide.astype(BF16), k[s], (((1,), (1,)), ((), ())), preferred_element_type=F32
            )
            own = jnp.sum(wide * nk_rows[s : s + 1, :], axis=1, keepdims=True)
            score_rows[s * heads : (s + 1) * heads, :] = jnp.where(
                lane < lens[s], scores * scale, -1e30
            )
            own_rows[s * heads : (s + 1) * heads, :] = own * scale

    def attend_values(lo, hi):
        part = slice(lo * heads, hi * heads)
        scores = score_rows[part, :]
        own = own_rows[part, :]
        highest = jnp.maximum(jnp.max(scores, axis=1, keepdims=True), own)
        terms = jnp.exp(scores - highest)
        own_term = jnp.exp(own - highest)
        total = jnp.sum(terms, axis=1, keepdims=True) + own_term
        weights = (terms / total).astype(BF16)
        own_weight = (own_term / total).astype(BF16).astype(F32)
        for s in range(lo, hi):
            at = (s - lo) * heads
            full = jnp.dot(weights[at : at + heads, :], v[s], preferred_element_type=F32)
            full = full + own_weight[at : at + heads, :] * nv_rows[s : s + 1, :]
            picked = full[:, 0:HEAD]
            for j in range(1, kv_heads):
                picked = jnp.where(head_of == j, full[:, j * HEAD : (j + 1) * HEAD], picked)
            att_rows[pl.ds(s, heads, stride=rows), :] = picked

    attend_scores(0, rows)

    for i in range(1, experts):
        send(i).wait_recv()
        relay(i).start()
        x_own[CAP * i : CAP * (i + 1), :] = arrived[i]
    loads[8].wait()
    hidden_part[...] = jnp.dot(x_own[...], win[0], preferred_element_type=F32)
    for i in range(experts):
        relay(i).wait_recv()
        x_other[CAP * i : CAP * (i + 1), :] = relayed[i]
    loads[9].wait()
    hidden = jnp.maximum(
        hidden_part[...] + jnp.dot(x_other[...], win[1], preferred_element_type=F32), 0.0
    ).astype(BF16)

    piece = half // RETURN_PIECES

    def part_copy(c):
        return pltpu.make_async_remote_copy(
            src_ref=part_send.at[c],
            dst_ref=part_recv.at[c],
            send_sem=part_ssem.at[c],
            recv_sem=part_rsem.at[c],
            device_id=(me, other),
            device_id_type=MESH,
        )

    def give_back(c, i):
        return pltpu.make_async_remote_copy(
            src_ref=ret.at[c, i],
            dst_ref=back.at[c, i],
            send_sem=ret_send.at[c, i],
            recv_sem=ret_recv.at[c, i],
            device_id=(partner(me, i), core),
            device_id_type=MESH,
        )

    loads[10].wait()
    for c in range(RETURN_PIECES):
        part_send[c] = jnp.dot(
            hidden, wout[0, :, c * piece : (c + 1) * piece], preferred_element_type=F32
        ).astype(BF16)
        part_copy(c).start()
    loads[11].wait()
    for c in range(RETURN_PIECES):
        cols = slice(c * piece, (c + 1) * piece)
        own_part = jnp.dot(hidden, wout[1, :, cols], preferred_element_type=F32)
        part_copy(c).wait_recv()
        ret2d[c] = (own_part + part_recv[c].astype(F32)).astype(BF16)
        for i in far_first:
            ret[c, i] = ret2d[c, CAP * i : CAP * (i + 1), :]
            give_back(c, i).start()
        back2d[0:CAP, cols] = ret2d[c, 0:CAP, :]

    loads[7].wait()
    attend_values(0, rows)
    for h in range(heads):
        att[:, h * HEAD : (h + 1) * HEAD] = att_rows[h * rows : (h + 1) * rows, :].astype(BF16)

    for c in range(RETURN_PIECES):
        cols = slice(c * piece, (c + 1) * piece)
        for i in range(1, experts):
            give_back(c, i).wait_recv()
            back2d[CAP * i : CAP * (i + 1), cols] = back[c, i]
        expert_out = jnp.dot(placed_t, back2d[:, cols], preferred_element_type=F32)
        at = pl.multiple_of(own_off + c * piece, piece)
        mixed[:, cols] = (tok[:, pl.ds(at, piece)].astype(F32) + expert_out).astype(BF16)

    for i in range(1, experts):
        send(i).wait_send()
    for i in range(experts):
        relay(i).wait_send()
    for c in range(RETURN_PIECES):
        part_copy(c).wait_send()
        for i in range(1, experts):
            give_back(c, i).wait_send()


def finish_kernel(mixed_in, att_in, mixed, att, sem):
    copies = [
        pltpu.make_async_copy(mixed_in, mixed, sem.at[0]),
        pltpu.make_async_copy(att_in, att, sem.at[1]),
    ]
    for copy in copies:
        copy.start()
    for copy in copies:
        copy.wait()


def shards(tokens, norm_gain, expert_ids, w_in, w_out, queries, keys, values, new_keys, new_values, lens):
    experts = lax.axis_size("expert")
    rows, width = tokens.shape
    half = width // 2
    inner = w_in.shape[2]
    slots = experts * CAP
    heads = queries.shape[1] // HEAD
    ctx = keys.shape[1]
    piece = half // RETURN_PIECES
    dma = pltpu.SemaphoreType.DMA
    ids = expert_ids.reshape(1, rows)
    hbm = pl.BlockSpec(memory_space=pltpu.HBM)
    vmem = pl.BlockSpec(memory_space=pltpu.VMEM)
    like = lambda a: pltpu.VMEM(a.shape, a.dtype)
    outs = (
            jax.ShapeDtypeStruct((rows, half), BF16),
            jax.ShapeDtypeStruct(queries.shape, BF16),
        )
    mixed, att = pl.pallas_call(
        functools.partial(step_kernel, experts),
        out_shape=(pltpu.VMEM((rows, half), BF16), pltpu.VMEM(queries.shape, BF16)),
        in_specs=[pl.BlockSpec(memory_space=pltpu.SMEM)] + [hbm] * 10,
        out_specs=(vmem, vmem),
        scratch_shapes=[
            like(tokens),
            like(norm_gain),
            like(ids),
            pltpu.VMEM((2, half, inner), BF16),
            pltpu.VMEM((2, inner, half), BF16),
            like(queries),
            like(keys),
            like(values),
            like(new_keys),
            like(new_values),
            pltpu.VMEM((slots, half), BF16),
            pltpu.VMEM((experts, CAP, half), BF16),
            pltpu.VMEM((experts, CAP, half), BF16),
            pltpu.VMEM((experts, CAP, half), BF16),
            pltpu.VMEM((slots, half), BF16),
            pltpu.VMEM((slots, half), BF16),
            pltpu.VMEM((slots, inner), F32),
            pltpu.VMEM((RETURN_PIECES, slots, piece), BF16),
            pltpu.VMEM((RETURN_PIECES, slots, piece), BF16),
            pltpu.VMEM((RETURN_PIECES, slots, piece), BF16),
            pltpu.VMEM((RETURN_PIECES, experts, CAP, piece), BF16),
            pltpu.VMEM((RETURN_PIECES, experts, CAP, piece), BF16),
            pltpu.VMEM((slots, half), BF16),
            pltpu.VMEM((heads * rows, HEAD), F32),
            pltpu.VMEM(new_keys.shape, F32),
            pltpu.VMEM(new_values.shape, F32),
            pltpu.VMEM((heads * rows, ctx), F32),
            pltpu.VMEM((heads * rows, 1), F32),
            pltpu.VMEM((heads * rows, HEAD), F32),
            dma((12,)),
            dma((experts,)),
            dma((experts,)),
            dma((experts,)),
            dma((experts,)),
            dma((RETURN_PIECES,)),
            dma((RETURN_PIECES,)),
            dma((RETURN_PIECES, experts)),
            dma((RETURN_PIECES, experts)),
        ],
        compiler_params=pltpu.CompilerParams(
            collective_id=0, has_side_effects=True, vmem_limit_bytes=60 * 1024 * 1024
        ),
    )(lens, tokens, norm_gain, ids, w_in, w_out, queries, keys, values, new_keys, new_values)
    return pl.pallas_call(
        finish_kernel,
        out_shape=outs,
        in_specs=[vmem, vmem],
        out_specs=(hbm, hbm),
        scratch_shapes=[dma((2,))],
        compiler_params=pltpu.CompilerParams(vmem_limit_bytes=1024 * 1024),
    )(mixed, att)


def solution(mesh):
    return jax.shard_map(
        shards,
        mesh=mesh,
        in_specs=(
            P("expert", None),
            P(),
            P("expert", None),
            P("expert", None, "mp"),
            P("expert", "mp", None),
            P("expert", "mp"),
            P("expert", None, "mp"),
            P("expert", None, "mp"),
            P("expert", "mp"),
            P("expert", "mp"),
            P("expert"),
        ),
        out_specs=(P("expert", "mp"), P("expert", "mp")),
        check_vma=False,
    )
```

```python
import functools

import jax
import jax.numpy as jnp
from jax import lax
from jax.experimental import pallas as pl
from jax.experimental.pallas import tpu as pltpu
from jax.sharding import PartitionSpec as P

HEAD = 128
CAP = 2
RETURN_PIECES = 1
PART_PIECES = 2
F32 = jnp.float32
BF16 = jnp.bfloat16
MESH = pl.DeviceIdType.MESH


def partner(me, i):
    bit = 1
    at = me
    while bit <= i:
        if i & bit:
            at = at + bit - 2 * bit * (me // bit % 2)
        bit *= 2
    return at


def step_kernel(
    experts,
    lens,
    tok_h,
    gain_h,
    ids_h,
    win_h,
    wout_h,
    q_h,
    k_h,
    v_h,
    nk_h,
    nv_h,
    mixed,
    att,
    tok,
    gain,
    ids,
    win,
    wout,
    q,
    k,
    v,
    nk,
    nv,
    out2d,
    outgoing,
    arrived,
    relayed,
    x_own,
    x_other,
    hidden_part,
    part_send,
    part_recv,
    ret2d,
    ret,
    back,
    back2d,
    q_rows,
    nk_rows,
    nv_rows,
    score_rows,
    own_rows,
    att_rows,
    load_sem,
    send_sem,
    recv_sem,
    relay_send,
    relay_recv,
    part_ssem,
    part_rsem,
    ret_send,
    ret_recv,
):
    rows, width = tok.shape
    half = width // 2
    me = lax.axis_index("expert")
    core = lax.axis_index("mp")
    other = 1 - core
    own_off = pl.multiple_of(core * half, half)
    other_off = pl.multiple_of(other * half, half)
    slots = experts * CAP
    far_first = range(experts - 1, 0, -1)

    loads = [
        pltpu.make_async_copy(src, dst, load_sem.at[n])
        for n, (src, dst) in enumerate(
            [
                (tok_h, tok),
                (ids_h, ids),
                (gain_h, gain),
                (q_h, q),
                (nk_h, nk),
                (nv_h, nv),
                (k_h, k),
                (v_h, v),
                (win_h.at[0, pl.ds(own_off, half), :], win.at[0]),
                (win_h.at[0, pl.ds(other_off, half), :], win.at[1]),
                (wout_h.at[0, :, pl.ds(other_off, half)], wout.at[0]),
                (wout_h.at[0, :, pl.ds(own_off, half)], wout.at[1]),
            ]
        )
    ]
    for load in loads[:3]:
        load.start()

    barrier = pltpu.get_barrier_semaphore()
    for i in far_first:
        pl.semaphore_signal(
            barrier, inc=1, device_id=(partner(me, i), core), device_id_type=MESH
        )
    pl.semaphore_signal(barrier, inc=1, device_id=(me, other), device_id_type=MESH)
    for load in loads[3:]:
        load.start()

    for load in loads[:3]:
        load.wait()
    whole = tok[...].astype(F32)
    inverse = lax.rsqrt(jnp.mean(whole * whole, axis=-1, keepdims=True) + 1e-05)
    mine = tok[:, pl.ds(own_off, half)].astype(F32)
    normed = (mine * inverse * gain[pl.ds(own_off, half)].astype(F32)[None, :]).astype(BF16)
    relative = jnp.bitwise_xor(ids[...], me)
    onehot = relative == lax.broadcasted_iota(jnp.int32, (experts, rows), 0)
    onehot = jnp.where(onehot, 1.0, 0.0)
    r_i = lax.broadcasted_iota(jnp.int32, (rows, rows), 0)
    c_i = lax.broadcasted_iota(jnp.int32, (rows, rows), 1)
    above = jnp.where(r_i < c_i, 1.0, 0.0).astype(BF16)
    earlier = jnp.dot(onehot.astype(BF16), above, preferred_element_type=F32)
    slot = jnp.sum(earlier * onehot, axis=0, keepdims=True)
    target = relative.astype(F32) * CAP + slot
    placed = jnp.where(
        target == lax.broadcasted_iota(jnp.int32, (slots, rows), 0).astype(F32), 1.0, 0.0
    ).astype(BF16)
    spread = jnp.where(r_i == c_i, target, 0.0).astype(BF16)
    target_cols = jnp.dot(spread, jnp.ones((rows, slots), BF16), preferred_element_type=F32)
    placed_t = jnp.where(
        target_cols == lax.broadcasted_iota(jnp.int32, (rows, slots), 1).astype(F32), 1.0, 0.0
    ).astype(BF16)
    out2d[...] = jnp.dot(placed, normed, preferred_element_type=F32).astype(BF16)
    for i in range(experts):
        outgoing[i] = out2d[CAP * i : CAP * (i + 1), :]

    pl.semaphore_wait(barrier, experts)

    def relay(i):
        return pltpu.make_async_remote_copy(
            src_ref=outgoing.at[0] if i == 0 else arrived.at[i],
            dst_ref=relayed.at[i],
            send_sem=relay_send.at[i],
            recv_sem=relay_recv.at[i],
            device_id=(me, other),
            device_id_type=MESH,
        )

    def send(i):
        return pltpu.make_async_remote_copy(
            src_ref=outgoing.at[i],
            dst_ref=arrived.at[i],
            send_sem=send_sem.at[i],
            recv_sem=recv_sem.at[i],
            device_id=(partner(me, i), core),
            device_id_type=MESH,
        )

    for i in far_first:
        send(i).start()
    relay(0).start()
    x_own[0:CAP, :] = out2d[0:CAP, :]

    kv_heads = nk.shape[1] // HEAD
    heads = q.shape[1] // HEAD
    group = heads // kv_heads
    ctx = k.shape[1]
    for load in loads[3:7]:
        load.wait()
    for h in range(heads):
        q_rows[h * rows : (h + 1) * rows, :] = q[:, h * HEAD : (h + 1) * HEAD].astype(F32)
    nk_rows[...] = nk[...].astype(F32)
    nv_rows[...] = nv[...].astype(F32)
    lane = lax.broadcasted_iota(jnp.int32, (heads, ctx), 1)
    head_of = lax.broadcasted_iota(jnp.int32, (heads, HEAD), 0) // group
    scale = HEAD ** (-0.5)

    def attend_scores(lo, hi):
        for s in range(lo, hi):
            q_s = q_rows[pl.ds(s, heads, stride=rows), :]
            wide = jnp.concatenate(
                [jnp.where(head_of == j, q_s, 0.0) for j in range(kv_heads)], axis=1
            )
            scores = lax.dot_general(
                wide.astype(BF16), k[s], (((1,), (1,)), ((), ())), preferred_element_type=F32
            )
            own = jnp.sum(wide * nk_rows[s : s + 1, :], axis=1, keepdims=True)
            score_rows[s * heads : (s + 1) * heads, :] = jnp.where(
                lane < lens[s], scores * scale, -1e30
            )
            own_rows[s * heads : (s + 1) * heads, :] = own * scale

    def attend_values(lo, hi):
        part = slice(lo * heads, hi * heads)
        scores = score_rows[part, :]
        own = own_rows[part, :]
        highest = jnp.maximum(jnp.max(scores, axis=1, keepdims=True), own)
        terms = jnp.exp(scores - highest)
        own_term = jnp.exp(own - highest)
        total = jnp.sum(terms, axis=1, keepdims=True) + own_term
        weights = (terms / total).astype(BF16)
        own_weight = (own_term / total).astype(BF16).astype(F32)
        for s in range(lo, hi):
            at = (s - lo) * heads
            full = jnp.dot(weights[at : at + heads, :], v[s], preferred_element_type=F32)
            full = full + own_weight[at : at + heads, :] * nv_rows[s : s + 1, :]
            picked = full[:, 0:HEAD]
            for j in range(1, kv_heads):
                picked = jnp.where(head_of == j, full[:, j * HEAD : (j + 1) * HEAD], picked)
            att_rows[pl.ds(s, heads, stride=rows), :] = picked

    attend_scores(0, rows)

    for i in range(1, experts):
        send(i).wait_recv()
        relay(i).start()
    for i in range(1, experts):
        x_own[CAP * i : CAP * (i + 1), :] = arrived[i]
    loads[8].wait()
    hidden_part[...] = jnp.dot(x_own[...], win[0], preferred_element_type=F32)
    for i in range(experts):
        relay(i).wait_recv()
        x_other[CAP * i : CAP * (i + 1), :] = relayed[i]
    loads[9].wait()
    hidden = jnp.maximum(
        hidden_part[...] + jnp.dot(x_other[...], win[1], preferred_element_type=F32), 0.0
    ).astype(BF16)

    piece = half // RETURN_PIECES
    part = half // PART_PIECES

    def part_copy(c):
        return pltpu.make_async_remote_copy(
            src_ref=part_send.at[c],
            dst_ref=part_recv.at[c],
            send_sem=part_ssem.at[c],
            recv_sem=part_rsem.at[c],
            device_id=(me, other),
            device_id_type=MESH,
        )

    def give_back(c, i):
        return pltpu.make_async_remote_copy(
            src_ref=ret.at[c, i],
            dst_ref=back.at[c, i],
            send_sem=ret_send.at[c, i],
            recv_sem=ret_recv.at[c, i],
            device_id=(partner(me, i), core),
            device_id_type=MESH,
        )

    loads[10].wait()
    for c in range(PART_PIECES):
        part_send[c] = jnp.dot(
            hidden, wout[0, :, c * part : (c + 1) * part], preferred_element_type=F32
        ).astype(BF16)
        part_copy(c).start()
    loads[11].wait()
    for c in range(PART_PIECES):
        cols = slice(c * part, (c + 1) * part)
        own_part = jnp.dot(hidden, wout[1, :, cols], preferred_element_type=F32)
        part_copy(c).wait_recv()
        ret2d[0, :, cols] = (own_part + part_recv[c].astype(F32)).astype(BF16)
    for i in far_first:
        ret[0, i] = ret2d[0, CAP * i : CAP * (i + 1), :]
        give_back(0, i).start()
    back2d[0:CAP, :] = ret2d[0, 0:CAP, :]

    loads[7].wait()
    attend_values(0, rows)
    for h in range(heads):
        att[:, h * HEAD : (h + 1) * HEAD] = att_rows[h * rows : (h + 1) * rows, :].astype(BF16)

    for c in range(RETURN_PIECES):
        cols = slice(c * piece, (c + 1) * piece)
        for i in range(1, experts):
            give_back(c, i).wait_recv()
            back2d[CAP * i : CAP * (i + 1), cols] = back[c, i]
        expert_out = jnp.dot(placed_t, back2d[:, cols], preferred_element_type=F32)
        at = pl.multiple_of(own_off + c * piece, piece)
        mixed[:, cols] = (tok[:, pl.ds(at, piece)].astype(F32) + expert_out).astype(BF16)

    for i in range(1, experts):
        send(i).wait_send()
    for i in range(experts):
        relay(i).wait_send()
    for c in range(PART_PIECES):
        part_copy(c).wait_send()
    for c in range(RETURN_PIECES):
        for i in range(1, experts):
            give_back(c, i).wait_send()


def finish_kernel(mixed_in, att_in, mixed, att, sem):
    copies = [
        pltpu.make_async_copy(mixed_in, mixed, sem.at[0]),
        pltpu.make_async_copy(att_in, att, sem.at[1]),
    ]
    for copy in copies:
        copy.start()
    for copy in copies:
        copy.wait()


def shards(tokens, norm_gain, expert_ids, w_in, w_out, queries, keys, values, new_keys, new_values, lens):
    experts = lax.axis_size("expert")
    rows, width = tokens.shape
    half = width // 2
    inner = w_in.shape[2]
    slots = experts * CAP
    heads = queries.shape[1] // HEAD
    ctx = keys.shape[1]
    piece = half // RETURN_PIECES
    dma = pltpu.SemaphoreType.DMA
    ids = expert_ids.reshape(1, rows)
    hbm = pl.BlockSpec(memory_space=pltpu.HBM)
    vmem = pl.BlockSpec(memory_space=pltpu.VMEM)
    like = lambda a: pltpu.VMEM(a.shape, a.dtype)
    outs = (
            jax.ShapeDtypeStruct((rows, half), BF16),
            jax.ShapeDtypeStruct(queries.shape, BF16),
        )
    mixed, att = pl.pallas_call(
        functools.partial(step_kernel, experts),
        out_shape=(pltpu.VMEM((rows, half), BF16), pltpu.VMEM(queries.shape, BF16)),
        in_specs=[pl.BlockSpec(memory_space=pltpu.SMEM)] + [hbm] * 10,
        out_specs=(vmem, vmem),
        scratch_shapes=[
            like(tokens),
            like(norm_gain),
            like(ids),
            pltpu.VMEM((2, half, inner), BF16),
            pltpu.VMEM((2, inner, half), BF16),
            like(queries),
            like(keys),
            like(values),
            like(new_keys),
            like(new_values),
            pltpu.VMEM((slots, half), BF16),
            pltpu.VMEM((experts, CAP, half), BF16),
            pltpu.VMEM((experts, CAP, half), BF16),
            pltpu.VMEM((experts, CAP, half), BF16),
            pltpu.VMEM((slots, half), BF16),
            pltpu.VMEM((slots, half), BF16),
            pltpu.VMEM((slots, inner), F32),
            pltpu.VMEM((PART_PIECES, slots, half // PART_PIECES), BF16),
            pltpu.VMEM((PART_PIECES, slots, half // PART_PIECES), BF16),
            pltpu.VMEM((RETURN_PIECES, slots, piece), BF16),
            pltpu.VMEM((RETURN_PIECES, experts, CAP, piece), BF16),
            pltpu.VMEM((RETURN_PIECES, experts, CAP, piece), BF16),
            pltpu.VMEM((slots, half), BF16),
            pltpu.VMEM((heads * rows, HEAD), F32),
            pltpu.VMEM(new_keys.shape, F32),
            pltpu.VMEM(new_values.shape, F32),
            pltpu.VMEM((heads * rows, ctx), F32),
            pltpu.VMEM((heads * rows, 1), F32),
            pltpu.VMEM((heads * rows, HEAD), F32),
            dma((12,)),
            dma((experts,)),
            dma((experts,)),
            dma((experts,)),
            dma((experts,)),
            dma((PART_PIECES,)),
            dma((PART_PIECES,)),
            dma((RETURN_PIECES, experts)),
            dma((RETURN_PIECES, experts)),
        ],
        compiler_params=pltpu.CompilerParams(
            collective_id=0, has_side_effects=True, vmem_limit_bytes=60 * 1024 * 1024
        ),
    )(lens, tokens, norm_gain, ids, w_in, w_out, queries, keys, values, new_keys, new_values)
    return pl.pallas_call(
        finish_kernel,
        out_shape=outs,
        in_specs=[vmem, vmem],
        out_specs=(hbm, hbm),
        scratch_shapes=[dma((2,))],
        compiler_params=pltpu.CompilerParams(vmem_limit_bytes=1024 * 1024),
    )(mixed, att)


def solution(mesh):
    return jax.shard_map(
        shards,
        mesh=mesh,
        in_specs=(
            P("expert", None),
            P(),
            P("expert", None),
            P("expert", None, "mp"),
            P("expert", "mp", None),
            P("expert", "mp"),
            P("expert", None, "mp"),
            P("expert", None, "mp"),
            P("expert", "mp"),
            P("expert", "mp"),
            P("expert"),
        ),
        out_specs=(P("expert", "mp"), P("expert", "mp")),
        check_vma=False,
    )
```
